32 devices in a mesh: pole: 2 (over y), row: 4 (over z), col: 4 (over x, core).
Axes of the slice: x: 2, y: 2, z: 4, core: 2. Of those that a mesh axis runs over, the one named last changes fastest.
Arguments:
- ainv_cc: bfloat16 [2048, 1024], P(('pole', 'row'), 'col'), parts along dimension 0, may hold values from -6 to 6
- factor: bfloat16 [4, 1024, 1024], P('pole', 'row', 'col'), parts along dimension 0, may hold values from -0.375 to 0.375
- inv_pivot: float32 [4, 1024, 1024], P('pole', 'row', 'col'), parts along dimension 0, may hold values from -6 to 6
- pattern: int32 [2, 8], replicated, may hold values from 0 to 1, as said below
Outputs:
- ainv_kc: bfloat16 [4, 1024, 1024], P('pole', 'col', 'row'), parts along dimension 0
- ainv_kk: float32 [4, 1024, 1024], P('pole', 'row', 'col'), parts along dimension 0
The draws below stay inside these ranges and needn't reach their ends.
There are 2 independent parts, one for each index of `pole`. The reference program is written for one: setup_inputs(seed, part) draws one part's arguments, and reference() takes and returns one part's arrays. A program takes and returns all parts, laid end to end along the dimension named above; an argument that names none is the same for every part. Nothing has to cross between parts.
Inputs may be any that keep to these rules, and one draw needn't show every extreme that they name: `pattern`: for each supernode, each aligned group of 2 consecutive blocks (blocks g * 2 to (g + 1) * 2 - 1) holds at most 1 nonzero blocks, and some group holds exactly 1.
All inputs are finite; a program needn't handle non-finite values.
Results may differ from the reference program's by a relative error of at most 0.012.
Values may be sent and summed in bfloat16 or wider, within the bound.
A program may use at most 64 MiB of HBM per device.

```python
import jax
import jax.numpy as jnp
from jax import lax

W = 1024
BLK = 128
SUPERS = 2
RB_DEV = 2
NZ_MOST = 1
ANC = 1024
NB = 8
N_COL = 4


def draw_pattern(key, part):
    groups = NB // RB_DEV
    first_key, second_key, third_key = jax.random.split(jax.random.fold_in(key, 17), 3)
    counts = jax.random.randint(first_key, (SUPERS, groups), 0, NZ_MOST + 1)
    forced = jax.random.randint(second_key, (SUPERS,), 0, groups)
    group_ids = jnp.arange(groups, dtype=jnp.int32)
    counts = jnp.where(group_ids[None, :] == forced[:, None], NZ_MOST, counts)
    scores = jax.random.randint(third_key, (SUPERS, groups, RB_DEV), 0, 1 << 20) * RB_DEV
    scores = scores + jnp.arange(RB_DEV, dtype=jnp.int32)[None, None, :]
    ranks = jnp.argsort(jnp.argsort(scores, axis=2), axis=2)
    marks = (ranks < counts[:, :, None]).astype(jnp.int32)
    return marks.reshape(SUPERS, NB)


def block_levels(rng, shape, cuts, smallest, largest):
    gain, own = 1.0, jax.random.fold_in(rng, 6)
    for position, blocks in cuts:
        steps = jnp.exp(jax.random.uniform(jax.random.fold_in(own, position), (blocks,), jnp.float32, smallest / len(cuts), largest / len(cuts)))
        gain = gain * jnp.repeat(steps, shape[position] // blocks).reshape([-1 if axis == position else 1 for axis in range(len(shape))])
    return gain


def gaussian(rng, extent, width, reach, cuts=(), held_as=jnp.bfloat16):
    values = width * jax.random.normal(rng, extent, jnp.float32)
    if cuts:
        values = values * block_levels(rng, extent, cuts, -0.22, 0.18)
    return jnp.clip(values, -reach, reach).astype(held_as)


def setup_inputs(seed: int = 0, part: int = 0) -> dict:
    key_list = jax.random.split(jax.random.key(seed), 5)
    part_splits = jax.random.split(jax.random.fold_in(key_list[4], part), 5)
    return {
        "ainv_cc": gaussian(part_splits[0], (ANC, ANC), 1.0, 6.0, ((0, 4), (1, 4))),
        "factor": gaussian(part_splits[1], (SUPERS, ANC, W), (ANC // 4) ** -0.5, 0.375, ((1, 4), (2, 4))),
        "inv_pivot": gaussian(part_splits[2], (SUPERS, W, W), 1.0, 6.0, ((1, 4), (2, 4)), jnp.float32),
        "pattern": draw_pattern(jax.random.fold_in(key_list[4], 71), part),
    }


def masked_factor(factor, pattern):
    row_marks = jnp.repeat(pattern, BLK, axis=1)
    return jnp.where(row_marks[:, :, None] > 0, factor, jnp.zeros_like(factor))


def reference(ainv_cc, factor, inv_pivot, pattern):
    masked = masked_factor(factor, pattern)
    group_rows = ANC // N_COL
    cross_list = []
    diag_list = []
    for super_index in range(SUPERS):
        total = jnp.zeros((W, ANC), jnp.float32)
        for column in range(N_COL):
            rows_part = masked[super_index, column * group_rows:(column + 1) * group_rows]
            ainv_part = ainv_cc[:, column * group_rows:(column + 1) * group_rows]
            term = lax.dot_general(rows_part, ainv_part, (((0,), (1,)), ((), ())), preferred_element_type=jnp.float32)
            rounded = lax.optimization_barrier(term.astype(jnp.bfloat16))
            total = total + rounded.astype(jnp.float32)
        cross = (-total).astype(jnp.bfloat16)
        update = lax.dot_general(masked[super_index], cross, (((0,), (1,)), ((), ())), preferred_element_type=jnp.float32)
        cross_list.append(cross)
        diag_list.append(inv_pivot[super_index] - update)
    return (jnp.stack(cross_list), jnp.stack(diag_list))
```

```python
import functools

import jax
import jax.numpy as jnp
from jax import lax
from jax.experimental import pallas as pl
from jax.experimental.pallas import tpu as pltpu
from jax.sharding import PartitionSpec as P

BLK = 128
SUPERS = 2
RB_DEV = 2


def spread(x, axis, root):
    mine = lax.axis_index(axis) == root
    return lax.psum(jnp.where(mine, x, jnp.zeros_like(x)), axis)


def body(ainv_cc, factor, inv_pivot, pattern):
    rows_here = factor.shape[1]
    width_part = factor.shape[2]
    per_col = lax.axis_size("row") // lax.axis_size("col")
    row_index = lax.axis_index("row")
    col_index = lax.axis_index("col")
    full_width = lax.all_gather(factor, "col", axis=2, tiled=True)
    full_cols = full_width.shape[2]
    own_marks = lax.dynamic_slice_in_dim(pattern, row_index * RB_DEV, RB_DEV, 1)
    blocks = full_width.reshape(SUPERS, RB_DEV, BLK, full_cols)
    masked = jnp.where(own_marks[:, :, None, None] > 0, blocks, jnp.zeros_like(blocks))
    local_factor = masked.reshape(SUPERS, rows_here, full_cols)
    received = []
    for section in range(per_col):
        received.append(spread(local_factor, "row", col_index * per_col + section))
    gathered_rows = jnp.concatenate(received, axis=1)
    left_list = [ainv_cc for super_index in range(SUPERS)]
    cross_list = []
    diag_list = []
    for super_index in range(SUPERS):
        rows_matrix = gathered_rows[super_index]
        operand = left_list[super_index]
        factor_rows = local_factor[super_index]

        def column_term(first_row, row_count, rows_matrix=rows_matrix, operand=operand):
            return lax.dot_general(
                rows_matrix, operand, (((0,), (1,)), ((), ())), preferred_element_type=jnp.float32
            )

        summed = lax.psum_scatter(
            column_term(jnp.int32(0), lax.axis_size("col") * width_part).astype(jnp.bfloat16),
            "col",
            scatter_dimension=0,
            tiled=True,
        ).astype(jnp.float32)
        cross_block = (-summed).astype(jnp.bfloat16)

        def diagonal_term(first_row, row_count, factor_rows=factor_rows, cross_block=cross_block):
            return lax.dot_general(
                factor_rows,
                cross_block,
                (((0,), (1,)), ((), ())),
                preferred_element_type=jnp.float32,
            )

        update = lax.psum_scatter(
            diagonal_term(
                jnp.int32(0), lax.axis_size("row") * (full_cols // lax.axis_size("row"))
            ).astype(jnp.bfloat16),
            "row",
            scatter_dimension=0,
            tiled=True,
        ).astype(jnp.float32)
        cross_list.append(cross_block)
        diag_list.append(inv_pivot[super_index] - update)
    return (jnp.stack(cross_list), jnp.stack(diag_list))


def remote(src, dst, send_sem, recv_sem, row, col):
    return pltpu.make_async_remote_copy(
        src_ref=src,
        dst_ref=dst,
        send_sem=send_sem,
        recv_sem=recv_sem,
        device_id={"row": row, "col": col},
        device_id_type=pl.DeviceIdType.MESH,
    )


def kernel(
    n, pat, f_ref, a_ref, p_ref, kc_ref, kk_ref,
    mc, mr, af, ac, y,
    zm_send, zm_recv, za_send, za_recv, pa_send, pa_recv, pc_send, pc_recv, pm_send, pm_recv,
):
    r = lax.axis_index("row")
    c = lax.axis_index("col")
    sib = c + 1 - 2 * lax.rem(c, 2)
    far = lax.rem(c + 2, n)
    far_sib = lax.rem(sib + 2, n)
    steps = [(d, t) for t in range(n - 1) for d in (1, -1)]

    def slot(d, t):
        return t * 2 + (0 if d == 1 else 1)

    def guard(d, t, sending):
        if sending:
            if d == 1:
                return jnp.logical_and(r >= t, r < n - 1)
            return jnp.logical_and(r <= n - 1 - t, r > 0)
        if d == 1:
            return r >= t + 1
        return r <= n - 2 - t

    def z_m(d, t):
        b, k = r - d * t, slot(d, t)
        return remote(mc.at[b], mc.at[b], zm_send.at[k], zm_recv.at[k], r + d, c)

    def z_a(d, t):
        b, k = r - d * t, slot(d, t)
        return remote(ac.at[b, c], ac.at[b, c], za_send.at[k], za_recv.at[k], r + d, c)

    def z_m_in(d, t):
        b, k = r - d * (t + 1), slot(d, t)
        return remote(mc.at[b], mc.at[b], zm_send.at[k], zm_recv.at[k], r - d, c)

    def z_a_in(d, t):
        b, k = r - d * (t + 1), slot(d, t)
        return remote(ac.at[b, c], ac.at[b, c], za_send.at[k], za_recv.at[k], r - d, c)

    def plane_a(j):
        col, block = ((sib, c), (far, c), (sib, far))[j]
        return remote(af.at[block], af.at[block], pa_send.at[j], pa_recv.at[j], r, col)

    def plane_a_in(j):
        block = (sib, far, far_sib)[j]
        return remote(af.at[block], af.at[block], pa_send.at[j], pa_recv.at[j], r, sib)

    def plane_c(b, k, j):
        col, block = ((sib, c), (far, c), (sib, far))[j]
        return remote(
            ac.at[b, block], ac.at[b, block], pc_send.at[k, j], pc_recv.at[k, j], r, col
        )

    def plane_c_in(b, k, j):
        block = (sib, far, far_sib)[j]
        return remote(
            ac.at[b, block], ac.at[b, block], pc_send.at[k, j], pc_recv.at[k, j], r, sib
        )

    def plane_m(b, k, j):
        return remote(mc.at[b], mr.at[b], pm_send.at[k, j], pm_recv.at[k], r, (sib, far)[j])

    def plane_m_on(b, k):
        return remote(mr.at[b], mr.at[b], pm_send.at[k, 0], pm_recv.at[k], r, sib)

    def plane_m_in(b, k):
        return remote(mr.at[b], mr.at[b], pm_send.at[k, 0], pm_recv.at[k], r, sib)

    is_root = c == r
    is_hop = far == r
    own = slot(-1, n - 2) + 1

    barrier = pltpu.get_barrier_semaphore()
    for col in (sib, far):
        pl.semaphore_signal(
            barrier, inc=1, device_id={"row": r, "col": col}, device_id_type=pl.DeviceIdType.MESH
        )
    for d in (1, -1):

        @pl.when(guard(d, 0, True))
        def _(d=d):
            pl.semaphore_signal(
                barrier,
                inc=1,
                device_id={"row": r + d, "col": c},
                device_id_type=pl.DeviceIdType.MESH,
            )

    half = f_ref.shape[1] // RB_DEV
    for s in range(SUPERS):
        first = pat[s, RB_DEV * r] > 0
        second = pat[s, RB_DEV * r + 1] > 0
        lower = f_ref[s, :half, :]
        mc[r, s] = jnp.where(
            second, f_ref[s, half:, :], jnp.where(first, lower, jnp.zeros_like(lower))
        )
        rows = jnp.where(second, a_ref[half:, :], a_ref[:half, :])
        ac[r, c, s] = jnp.where(pat[s, RB_DEV * c + 1] > 0, rows[:, half:], rows[:, :half])
    af[c] = a_ref[...]

    pl.semaphore_wait(barrier, 2 + (r > 0).astype(jnp.int32) + (r < n - 1).astype(jnp.int32))

    for copy_of in (z_m, z_a):
        for d in (1, -1):

            @pl.when(guard(d, 0, True))
            def _(d=d, copy_of=copy_of):
                copy_of(d, 0).start()

    plane_a(1).start()
    plane_a(0).start()

    @pl.when(is_root)
    def _():
        plane_m(r, own, 1).start()
        plane_m(r, own, 0).start()
        mr[r] = mc[r]

    plane_a_in(1).wait_recv()
    plane_a(2).start()

    @pl.when(is_hop)
    def _():
        plane_m_in(r, own).wait_recv()
        plane_m_on(r, own).start()

    def relay(d, t):
        b, k = r - d * (t + 1), slot(d, t)

        @pl.when(guard(d, t, False))
        def _():
            plane_c_in(b, k, 1).wait_recv()
            plane_c(b, k, 2).start()

            @pl.when(is_hop)
            def _():
                plane_m_in(b, k).wait_recv()
                plane_m_on(b, k).start()

    for t in range(n - 1):
        for d in (1, -1):
            b, k = r - d * (t + 1), slot(d, t)

            @pl.when(guard(d, t, False))
            def _(d=d, t=t, b=b, k=k):
                z_m_in(d, t).wait_recv()
                if t + 1 < n - 1:

                    @pl.when(guard(d, t + 1, True))
                    def _():
                        z_m(d, t + 1).start()

                @pl.when(is_root)
                def _():
                    plane_m(b, k, 1).start()
                    plane_m(b, k, 0).start()

                z_a_in(d, t).wait_recv()
                if t + 1 < n - 1:

                    @pl.when(guard(d, t + 1, True))
                    def _():
                        z_a(d, t + 1).start()

                plane_c(b, k, 1).start()
                plane_c(b, k, 0).start()

        if t > 0:
            for d in (1, -1):
                relay(d, t - 1)
    for d in (1, -1):
        relay(d, n - 2)

    plane_a_in(0).wait_recv()
    plane_a_in(2).wait_recv()
    width = mc.shape[3]
    depth = n * half
    for s in range(SUPERS):
        columns = mc[:, s].reshape(depth, width)
        left = jnp.concatenate(
            [
                jnp.where(pat[s, RB_DEV * g + 1] > 0, af[g, :, half:], af[g, :, :half])
                for g in range(n)
            ],
            axis=1,
        )
        x = jnp.dot(left, columns, preferred_element_type=jnp.float32)
        kc_ref[s] = (-x).T.astype(jnp.bfloat16)
        y[r, s] = jnp.where(pat[s, RB_DEV * r + 1] > 0, x[half:], x[:half]).astype(jnp.bfloat16)

    for d, t in steps:
        b, k = r - d * (t + 1), slot(d, t)

        @pl.when(guard(d, t, False))
        def _(b=b, k=k):
            plane_c_in(b, k, 0).wait_recv()
            plane_c_in(b, k, 2).wait_recv()

    for off in range(1, n):
        b = lax.rem(r + off, n)
        for s in range(SUPERS):
            left = jnp.concatenate([ac[b, g, s] for g in range(n)], axis=1)
            y[b, s] = jnp.dot(
                left, mc[:, s].reshape(depth, width), preferred_element_type=jnp.float32
            ).astype(jnp.bfloat16)

    @pl.when(is_root)
    def _():
        for off in range(1, n):
            b = lax.rem(r + off, n)
            mr[b] = mc[b]

    is_leaf = jnp.logical_and(jnp.logical_not(is_root), jnp.logical_not(is_hop))

    @pl.when(is_leaf)
    def _():
        plane_m_in(r, own).wait_recv()

    for d, t in steps:
        b, k = r - d * (t + 1), slot(d, t)

        @pl.when(jnp.logical_and(is_leaf, guard(d, t, False)))
        def _(b=b, k=k):
            plane_m_in(b, k).wait_recv()

    for s in range(SUPERS):
        kk_ref[s] = p_ref[s] + lax.dot_general(
            mr[:, s].reshape(depth, width),
            y[:, s].reshape(depth, width),
            (((0,), (0,)), ((), ())),
            preferred_element_type=jnp.float32,
        )

    for d, t in steps:

        @pl.when(guard(d, t, True))
        def _(d=d, t=t):
            z_m(d, t).wait_send()
            z_a(d, t).wait_send()

        @pl.when(guard(d, t, False))
        def _(d=d, t=t):
            b, k = r - d * (t + 1), slot(d, t)
            for j in range(3):
                plane_c(b, k, j).wait_send()

            @pl.when(is_root)
            def _():
                plane_m(b, k, 0).wait_send()
                plane_m(b, k, 1).wait_send()

            @pl.when(is_hop)
            def _():
                plane_m_on(b, k).wait_send()

    for j in range(3):
        plane_a(j).wait_send()

    @pl.when(is_root)
    def _():
        plane_m(r, own, 0).wait_send()
        plane_m(r, own, 1).wait_send()

    @pl.when(is_hop)
    def _():
        plane_m_on(r, own).wait_send()


def body_kernel(n, ainv_cc, factor, inv_pivot, pattern):
    rows, width = factor.shape[1], factor.shape[2]
    half = rows // RB_DEV
    slots = 2 * (n - 1)
    vmem = pl.BlockSpec(memory_space=pltpu.VMEM)
    dma = pltpu.SemaphoreType.DMA
    return pl.pallas_call(
        functools.partial(kernel, n),
        out_shape=(
            jax.ShapeDtypeStruct((SUPERS, width, rows), jnp.bfloat16),
            jax.ShapeDtypeStruct(inv_pivot.shape, jnp.float32),
        ),
        in_specs=[pl.BlockSpec(memory_space=pltpu.SMEM), vmem, vmem, vmem],
        out_specs=(vmem, vmem),
        scratch_shapes=[
            pltpu.VMEM((n, SUPERS, half, width), jnp.bfloat16),
            pltpu.VMEM((n, SUPERS, half, width), jnp.bfloat16),
            pltpu.VMEM((n,) + ainv_cc.shape, jnp.bfloat16),
            pltpu.VMEM((n, n, SUPERS, half, half), jnp.bfloat16),
            pltpu.VMEM((n, SUPERS, half, width), jnp.bfloat16),
            dma((slots,)), dma((slots,)), dma((slots,)), dma((slots,)),
            dma((3,)), dma((3,)),
            dma((slots, 3)), dma((slots, 3)),
            dma((slots + 1, 2)), dma((slots + 1,)),
        ],
        compiler_params=pltpu.CompilerParams(
            collective_id=0, has_side_effects=True, vmem_limit_bytes=32 << 20
        ),
        cost_estimate=pl.CostEstimate(
            flops=2 * SUPERS * 3 * width * rows * n * half,
            bytes_accessed=8 * rows * width * SUPERS,
            transcendentals=0,
        ),
    )(pattern, factor, ainv_cc, inv_pivot)


def solution(mesh):
    placed = (P(("pole", "row"), "col"), P("pole", "row", "col"), P("pole", "row", "col"), P())
    rows, cols = mesh.shape["row"], mesh.shape["col"]
    fits = rows == cols and cols == 4
    return jax.shard_map(
        functools.partial(body_kernel, cols) if fits else body,
        mesh=mesh,
        in_specs=placed,
        out_specs=(P("pole", "col", "row"), P("pole", "row", "col")),
        check_vma=False,
    )
```

```python
import functools

import jax
import jax.numpy as jnp
from jax import lax
from jax.experimental import pallas as pl
from jax.experimental.pallas import tpu as pltpu
from jax.sharding import PartitionSpec as P

BLK = 128
SUPERS = 2
RB_DEV = 2


def spread(x, axis, root):
    mine = lax.axis_index(axis) == root
    return lax.psum(jnp.where(mine, x, jnp.zeros_like(x)), axis)


def body(ainv_cc, factor, inv_pivot, pattern):
    rows_here = factor.shape[1]
    width_part = factor.shape[2]
    per_col = lax.axis_size("row") // lax.axis_size("col")
    row_index = lax.axis_index("row")
    col_index = lax.axis_index("col")
    full_width = lax.all_gather(factor, "col", axis=2, tiled=True)
    full_cols = full_width.shape[2]
    own_marks = lax.dynamic_slice_in_dim(pattern, row_index * RB_DEV, RB_DEV, 1)
    blocks = full_width.reshape(SUPERS, RB_DEV, BLK, full_cols)
    masked = jnp.where(own_marks[:, :, None, None] > 0, blocks, jnp.zeros_like(blocks))
    local_factor = masked.reshape(SUPERS, rows_here, full_cols)
    received = []
    for section in range(per_col):
        received.append(spread(local_factor, "row", col_index * per_col + section))
    gathered_rows = jnp.concatenate(received, axis=1)
    left_list = [ainv_cc for super_index in range(SUPERS)]
    cross_list = []
    diag_list = []
    for super_index in range(SUPERS):
        rows_matrix = gathered_rows[super_index]
        operand = left_list[super_index]
        factor_rows = local_factor[super_index]

        def column_term(first_row, row_count, rows_matrix=rows_matrix, operand=operand):
            return lax.dot_general(
                rows_matrix, operand, (((0,), (1,)), ((), ())), preferred_element_type=jnp.float32
            )

        summed = lax.psum_scatter(
            column_term(jnp.int32(0), lax.axis_size("col") * width_part).astype(jnp.bfloat16),
            "col",
            scatter_dimension=0,
            tiled=True,
        ).astype(jnp.float32)
        cross_block = (-summed).astype(jnp.bfloat16)

        def diagonal_term(first_row, row_count, factor_rows=factor_rows, cross_block=cross_block):
            return lax.dot_general(
                factor_rows,
                cross_block,
                (((0,), (1,)), ((), ())),
                preferred_element_type=jnp.float32,
            )

        update = lax.psum_scatter(
            diagonal_term(
                jnp.int32(0), lax.axis_size("row") * (full_cols // lax.axis_size("row"))
            ).astype(jnp.bfloat16),
            "row",
            scatter_dimension=0,
            tiled=True,
        ).astype(jnp.float32)
        cross_list.append(cross_block)
        diag_list.append(inv_pivot[super_index] - update)
    return (jnp.stack(cross_list), jnp.stack(diag_list))


def remote(src, dst, send_sem, recv_sem, row, col):
    return pltpu.make_async_remote_copy(
        src_ref=src,
        dst_ref=dst,
        send_sem=send_sem,
        recv_sem=recv_sem,
        device_id={"row": row, "col": col},
        device_id_type=pl.DeviceIdType.MESH,
    )


def kernel(
    n, pat_hbm, f_hbm, a_hbm, p_hbm, kc_ref, kk_ref,
    pat, f_ref, a_ref, mc, mr, af, ac, y, load_sem,
    zm_send, zm_recv, za_send, za_recv, pa_send, pa_recv, pc_send, pc_recv, pm_send, pm_recv,
):
    r = lax.axis_index("row")
    c = lax.axis_index("col")
    sib = c + 1 - 2 * lax.rem(c, 2)
    far = lax.rem(c + 2, n)
    far_sib = lax.rem(sib + 2, n)
    steps = [(d, t) for t in range(n - 1) for d in (1, -1)]

    def slot(d, t):
        return t * 2 + (0 if d == 1 else 1)

    def guard(d, t, sending):
        if sending:
            if d == 1:
                return jnp.logical_and(r >= t, r < n - 1)
            return jnp.logical_and(r <= n - 1 - t, r > 0)
        if d == 1:
            return r >= t + 1
        return r <= n - 2 - t

    def z_m(d, t, s):
        b, k = r - d * t, slot(d, t)
        return remote(mc.at[b, s], mc.at[b, s], zm_send.at[k, s], zm_recv.at[k, s], r + d, c)

    def z_a(d, t):
        b, k = r - d * t, slot(d, t)
        return remote(ac.at[b, c], ac.at[b, c], za_send.at[k], za_recv.at[k], r + d, c)

    def z_m_in(d, t, s):
        b, k = r - d * (t + 1), slot(d, t)
        return remote(mc.at[b, s], mc.at[b, s], zm_send.at[k, s], zm_recv.at[k, s], r - d, c)

    def z_a_in(d, t):
        b, k = r - d * (t + 1), slot(d, t)
        return remote(ac.at[b, c], ac.at[b, c], za_send.at[k], za_recv.at[k], r - d, c)

    def plane_a(j):
        col, block = ((sib, c), (far, c), (sib, far))[j]
        return remote(af.at[block], af.at[block], pa_send.at[j], pa_recv.at[j], r, col)

    def plane_a_in(j):
        block = (sib, far, far_sib)[j]
        return remote(af.at[block], af.at[block], pa_send.at[j], pa_recv.at[j], r, sib)

    def plane_c(b, k, j):
        col, block = ((sib, c), (far, c), (sib, far))[j]
        return remote(
            ac.at[b, block], ac.at[b, block], pc_send.at[k, j], pc_recv.at[k, j], r, col
        )

    def plane_c_in(b, k, j):
        block = (sib, far, far_sib)[j]
        return remote(
            ac.at[b, block], ac.at[b, block], pc_send.at[k, j], pc_recv.at[k, j], r, sib
        )

    def plane_m(b, k, s, j):
        return remote(
            mc.at[b, s], mr.at[b, s], pm_send.at[k, s, j], pm_recv.at[k, s], r, (sib, far)[j]
        )

    def plane_m_on(b, k, s):
        return remote(mr.at[b, s], mr.at[b, s], pm_send.at[k, s, 0], pm_recv.at[k, s], r, sib)

    plane_m_in = plane_m_on

    is_root = c == r
    is_hop = far == r
    own = slot(-1, n - 2) + 1

    loads = [
        pltpu.make_async_copy(src, dst, load_sem.at[i])
        for i, (src, dst) in enumerate(
            ((pat_hbm, pat), (f_hbm, f_ref), (a_hbm, a_ref), (p_hbm, kk_ref))
        )
    ]
    for load in loads:
        load.start()

    barrier = pltpu.get_barrier_semaphore()
    for col in (sib, far):
        pl.semaphore_signal(
            barrier, inc=1, device_id={"row": r, "col": col}, device_id_type=pl.DeviceIdType.MESH
        )
    for d in (1, -1):

        @pl.when(guard(d, 0, True))
        def _(d=d):
            pl.semaphore_signal(
                barrier,
                inc=1,
                device_id={"row": r + d, "col": c},
                device_id_type=pl.DeviceIdType.MESH,
            )

    half = f_ref.shape[1] // RB_DEV
    for load in loads[:3]:
        load.wait()
    for s in range(SUPERS):
        first = pat[s, RB_DEV * r] > 0
        second = pat[s, RB_DEV * r + 1] > 0
        lower = f_ref[s, :half, :]
        mc[r, s] = jnp.where(
            second, f_ref[s, half:, :], jnp.where(first, lower, jnp.zeros_like(lower))
        )
        rows = jnp.where(second, a_ref[half:, :], a_ref[:half, :])
        ac[r, c, s] = jnp.where(pat[s, RB_DEV * c + 1] > 0, rows[:, half:], rows[:, :half])
    af[c] = a_ref[...]

    pl.semaphore_wait(barrier, 2 + (r > 0).astype(jnp.int32) + (r < n - 1).astype(jnp.int32))

    for s in range(SUPERS):
        for d in (1, -1):

            @pl.when(guard(d, 0, True))
            def _(d=d, s=s):
                z_m(d, 0, s).start()

    for d in (1, -1):

        @pl.when(guard(d, 0, True))
        def _(d=d):
            z_a(d, 0).start()

    plane_a(1).start()
    plane_a(0).start()

    @pl.when(is_root)
    def _():
        for s in range(SUPERS):
            plane_m(r, own, s, 1).start()
            plane_m(r, own, s, 0).start()
        mr[r] = mc[r]

    def relay(d, t):
        b, k = r - d * (t + 1), slot(d, t)

        @pl.when(guard(d, t, False))
        def _():
            @pl.when(is_hop)
            def _():
                for s in range(SUPERS):
                    plane_m_in(b, k, s).wait_recv()
                    plane_m_on(b, k, s).start()

            plane_c_in(b, k, 1).wait_recv()
            plane_c(b, k, 2).start()

    for t in range(n - 1):
        for s in range(SUPERS):
            for d in (1, -1):
                b, k = r - d * (t + 1), slot(d, t)

                @pl.when(guard(d, t, False))
                def _(d=d, t=t, b=b, k=k, s=s):
                    z_m_in(d, t, s).wait_recv()
                    if t + 1 < n - 1:

                        @pl.when(guard(d, t + 1, True))
                        def _():
                            z_m(d, t + 1, s).start()

                    @pl.when(is_root)
                    def _():
                        plane_m(b, k, s, 1).start()
                        plane_m(b, k, s, 0).start()

        for d in (1, -1):
            b, k = r - d * (t + 1), slot(d, t)

            @pl.when(guard(d, t, False))
            def _(d=d, t=t, b=b, k=k):
                z_a_in(d, t).wait_recv()
                if t + 1 < n - 1:

                    @pl.when(guard(d, t + 1, True))
                    def _():
                        z_a(d, t + 1).start()

                plane_c(b, k, 1).start()
                plane_c(b, k, 0).start()

        if t == 0:
            plane_a_in(1).wait_recv()
            plane_a(2).start()

            @pl.when(is_hop)
            def _():
                for s in range(SUPERS):
                    plane_m_in(r, own, s).wait_recv()
                    plane_m_on(r, own, s).start()

        else:
            for d in (1, -1):
                relay(d, t - 1)
    for d in (1, -1):
        relay(d, n - 2)

    plane_a_in(0).wait_recv()
    plane_a_in(2).wait_recv()
    width = mc.shape[3]
    depth = n * half
    for s in range(SUPERS):
        columns = mc[:, s].reshape(depth, width)
        left = jnp.concatenate(
            [
                jnp.where(pat[s, RB_DEV * g + 1] > 0, af[g, :, half:], af[g, :, :half])
                for g in range(n)
            ],
            axis=1,
        )
        x = jnp.dot(left, columns, preferred_element_type=jnp.float32)
        kc_ref[s] = (-x).T.astype(jnp.bfloat16)
        y[r, s] = jnp.where(pat[s, RB_DEV * r + 1] > 0, x[half:], x[:half]).astype(jnp.bfloat16)

    for d, t in steps:
        b, k = r - d * (t + 1), slot(d, t)

        @pl.when(guard(d, t, False))
        def _(b=b, k=k):
            plane_c_in(b, k, 0).wait_recv()
            plane_c_in(b, k, 2).wait_recv()

    for off in range(1, n):
        b = lax.rem(r + off, n)
        for s in range(SUPERS):
            left = jnp.concatenate([ac[b, g, s] for g in range(n)], axis=1)
            y[b, s] = jnp.dot(
                left, mc[:, s].reshape(depth, width), preferred_element_type=jnp.float32
            ).astype(jnp.bfloat16)

    @pl.when(is_root)
    def _():
        for off in range(1, n):
            b = lax.rem(r + off, n)
            mr[b] = mc[b]

    is_leaf = jnp.logical_and(jnp.logical_not(is_root), jnp.logical_not(is_hop))

    @pl.when(is_leaf)
    def _():
        for s in range(SUPERS):
            plane_m_in(r, own, s).wait_recv()

    for d, t in steps:
        b, k = r - d * (t + 1), slot(d, t)

        @pl.when(jnp.logical_and(is_leaf, guard(d, t, False)))
        def _(b=b, k=k):
            for s in range(SUPERS):
                plane_m_in(b, k, s).wait_recv()

    loads[3].wait()
    for s in range(SUPERS):
        kk_ref[s] = kk_ref[s] + lax.dot_general(
            mr[:, s].reshape(depth, width),
            y[:, s].reshape(depth, width),
            (((0,), (0,)), ((), ())),
            preferred_element_type=jnp.float32,
        )

    for d, t in steps:

        @pl.when(guard(d, t, True))
        def _(d=d, t=t):
            for s in range(SUPERS):
                z_m(d, t, s).wait_send()
            z_a(d, t).wait_send()

        @pl.when(guard(d, t, False))
        def _(d=d, t=t):
            b, k = r - d * (t + 1), slot(d, t)
            for j in range(3):
                plane_c(b, k, j).wait_send()

            @pl.when(is_root)
            def _():
                for s in range(SUPERS):
                    plane_m(b, k, s, 0).wait_send()
                    plane_m(b, k, s, 1).wait_send()

            @pl.when(is_hop)
            def _():
                for s in range(SUPERS):
                    plane_m_on(b, k, s).wait_send()

    for j in range(3):
        plane_a(j).wait_send()

    @pl.when(is_root)
    def _():
        for s in range(SUPERS):
            plane_m(r, own, s, 0).wait_send()
            plane_m(r, own, s, 1).wait_send()

    @pl.when(is_hop)
    def _():
        for s in range(SUPERS):
            plane_m_on(r, own, s).wait_send()


def body_kernel(n, ainv_cc, factor, inv_pivot, pattern):
    rows, width = factor.shape[1], factor.shape[2]
    half = rows // RB_DEV
    slots = 2 * (n - 1)
    vmem = pl.BlockSpec(memory_space=pltpu.VMEM)
    dma = pltpu.SemaphoreType.DMA
    return pl.pallas_call(
        functools.partial(kernel, n),
        out_shape=(
            jax.ShapeDtypeStruct((SUPERS, width, rows), jnp.bfloat16),
            jax.ShapeDtypeStruct(inv_pivot.shape, jnp.float32),
        ),
        in_specs=[pl.BlockSpec(memory_space=pltpu.MemorySpace.HBM)] * 4,
        out_specs=(vmem, vmem),
        scratch_shapes=[
            pltpu.SMEM(pattern.shape, jnp.int32),
            pltpu.VMEM(factor.shape, jnp.bfloat16),
            pltpu.VMEM(ainv_cc.shape, jnp.bfloat16),
            pltpu.VMEM((n, SUPERS, half, width), jnp.bfloat16),
            pltpu.VMEM((n, SUPERS, half, width), jnp.bfloat16),
            pltpu.VMEM((n,) + ainv_cc.shape, jnp.bfloat16),
            pltpu.VMEM((n, n, SUPERS, half, half), jnp.bfloat16),
            pltpu.VMEM((n, SUPERS, half, width), jnp.bfloat16),
            dma((4,)),
            dma((slots, SUPERS)), dma((slots, SUPERS)), dma((slots,)), dma((slots,)),
            dma((3,)), dma((3,)),
            dma((slots, 3)), dma((slots, 3)),
            dma((slots + 1, SUPERS, 2)), dma((slots + 1, SUPERS)),
        ],
        compiler_params=pltpu.CompilerParams(
            collective_id=0, has_side_effects=True, vmem_limit_bytes=32 << 20
        ),
        cost_estimate=pl.CostEstimate(
            flops=2 * SUPERS * 3 * width * rows * n * half,
            bytes_accessed=8 * rows * width * SUPERS,
            transcendentals=0,
        ),
    )(
        *(
            pltpu.with_memory_space_constraint(x, pltpu.MemorySpace.HBM)
            for x in (pattern, factor, ainv_cc, inv_pivot)
        )
    )


def solution(mesh):
    placed = (P(("pole", "row"), "col"), P("pole", "row", "col"), P("pole", "row", "col"), P())
    rows, cols = mesh.shape["row"], mesh.shape["col"]
    fits = rows == cols and cols == 4
    return jax.shard_map(
        functools.partial(body_kernel, cols) if fits else body,
        mesh=mesh,
        in_specs=placed,
        out_specs=(P("pole", "col", "row"), P("pole", "row", "col")),
        check_vma=False,
    )
```

```python
import functools

import jax
import jax.numpy as jnp
from jax import lax
from jax.experimental import pallas as pl
from jax.experimental.pallas import tpu as pltpu
from jax.sharding import PartitionSpec as P

BLK = 128
SUPERS = 2
RB_DEV = 2


def spread(x, axis, root):
    mine = lax.axis_index(axis) == root
    return lax.psum(jnp.where(mine, x, jnp.zeros_like(x)), axis)


def body(ainv_cc, factor, inv_pivot, pattern):
    rows_here = factor.shape[1]
    width_part = factor.shape[2]
    per_col = lax.axis_size("row") // lax.axis_size("col")
    row_index = lax.axis_index("row")
    col_index = lax.axis_index("col")
    full_width = lax.all_gather(factor, "col", axis=2, tiled=True)
    full_cols = full_width.shape[2]
    own_marks = lax.dynamic_slice_in_dim(pattern, row_index * RB_DEV, RB_DEV, 1)
    blocks = full_width.reshape(SUPERS, RB_DEV, BLK, full_cols)
    masked = jnp.where(own_marks[:, :, None, None] > 0, blocks, jnp.zeros_like(blocks))
    local_factor = masked.reshape(SUPERS, rows_here, full_cols)
    received = []
    for section in range(per_col):
        received.append(spread(local_factor, "row", col_index * per_col + section))
    gathered_rows = jnp.concatenate(received, axis=1)
    left_list = [ainv_cc for super_index in range(SUPERS)]
    cross_list = []
    diag_list = []
    for super_index in range(SUPERS):
        rows_matrix = gathered_rows[super_index]
        operand = left_list[super_index]
        factor_rows = local_factor[super_index]

        def column_term(first_row, row_count, rows_matrix=rows_matrix, operand=operand):
            return lax.dot_general(
                rows_matrix, operand, (((0,), (1,)), ((), ())), preferred_element_type=jnp.float32
            )

        summed = lax.psum_scatter(
            column_term(jnp.int32(0), lax.axis_size("col") * width_part).astype(jnp.bfloat16),
            "col",
            scatter_dimension=0,
            tiled=True,
        ).astype(jnp.float32)
        cross_block = (-summed).astype(jnp.bfloat16)

        def diagonal_term(first_row, row_count, factor_rows=factor_rows, cross_block=cross_block):
            return lax.dot_general(
                factor_rows,
                cross_block,
                (((0,), (1,)), ((), ())),
                preferred_element_type=jnp.float32,
            )

        update = lax.psum_scatter(
            diagonal_term(
                jnp.int32(0), lax.axis_size("row") * (full_cols // lax.axis_size("row"))
            ).astype(jnp.bfloat16),
            "row",
            scatter_dimension=0,
            tiled=True,
        ).astype(jnp.float32)
        cross_list.append(cross_block)
        diag_list.append(inv_pivot[super_index] - update)
    return (jnp.stack(cross_list), jnp.stack(diag_list))


def remote(src, dst, send_sem, recv_sem, row, col):
    return pltpu.make_async_remote_copy(
        src_ref=src,
        dst_ref=dst,
        send_sem=send_sem,
        recv_sem=recv_sem,
        device_id={"row": row, "col": col},
        device_id_type=pl.DeviceIdType.MESH,
    )


def kernel(
    n, pat_hbm, f_hbm, a_hbm, p_hbm, kc_ref, kk_ref,
    pat, f_ref, a_ref, mc, mr, af, ac, y, load_sem,
    zm_send, zm_recv, za_send, za_recv, pa_send, pa_recv, pc_send, pc_recv, pm_send, pm_recv,
):
    r = lax.axis_index("row")
    c = lax.axis_index("col")
    sib = c + 1 - 2 * lax.rem(c, 2)
    far = lax.rem(c + 2, n)
    far_sib = lax.rem(sib + 2, n)
    steps = [(d, t) for t in range(n - 1) for d in (1, -1)]

    def slot(d, t):
        return t * 2 + (0 if d == 1 else 1)

    def guard(d, t, sending):
        if sending:
            if d == 1:
                return jnp.logical_and(r >= t, r < n - 1)
            return jnp.logical_and(r <= n - 1 - t, r > 0)
        if d == 1:
            return r >= t + 1
        return r <= n - 2 - t

    def z_m(d, t, s):
        b, k = r - d * t, slot(d, t)
        return remote(mc.at[b, s], mc.at[b, s], zm_send.at[k, s], zm_recv.at[k, s], r + d, c)

    def z_a(d, t):
        b, k = r - d * t, slot(d, t)
        return remote(ac.at[b, c], ac.at[b, c], za_send.at[k], za_recv.at[k], r + d, c)

    def z_m_in(d, t, s):
        b, k = r - d * (t + 1), slot(d, t)
        return remote(mc.at[b, s], mc.at[b, s], zm_send.at[k, s], zm_recv.at[k, s], r - d, c)

    def z_a_in(d, t):
        b, k = r - d * (t + 1), slot(d, t)
        return remote(ac.at[b, c], ac.at[b, c], za_send.at[k], za_recv.at[k], r - d, c)

    def plane_a(j):
        col, block = ((sib, c), (far, c), (sib, far))[j]
        return remote(af.at[block], af.at[block], pa_send.at[j], pa_recv.at[j], r, col)

    def plane_a_in(j):
        block = (sib, far, far_sib)[j]
        return remote(af.at[block], af.at[block], pa_send.at[j], pa_recv.at[j], r, sib)

    def plane_c(b, k, j):
        col, block = ((sib, c), (far, c), (sib, far))[j]
        return remote(
            ac.at[b, block], ac.at[b, block], pc_send.at[k, j], pc_recv.at[k, j], r, col
        )

    def plane_c_in(b, k, j):
        block = (sib, far, far_sib)[j]
        return remote(
            ac.at[b, block], ac.at[b, block], pc_send.at[k, j], pc_recv.at[k, j], r, sib
        )

    def plane_m(b, k, s, j):
        return remote(
            mc.at[b, s], mr.at[b, s], pm_send.at[k, s, j], pm_recv.at[k, s], r, (sib, far)[j]
        )

    def plane_m_on(b, k, s):
        return remote(mr.at[b, s], mr.at[b, s], pm_send.at[k, s, 0], pm_recv.at[k, s], r, sib)

    plane_m_in = plane_m_on

    is_root = c == r
    is_hop = far == r
    own = slot(-1, n - 2) + 1

    loads = [
        pltpu.make_async_copy(src, dst, load_sem.at[i])
        for i, (src, dst) in enumerate(
            ((pat_hbm, pat), (f_hbm, f_ref), (a_hbm, a_ref), (p_hbm, kk_ref))
        )
    ]
    for load in loads:
        load.start()

    barrier = pltpu.get_barrier_semaphore()
    for col in (sib, far):
        pl.semaphore_signal(
            barrier, inc=1, device_id={"row": r, "col": col}, device_id_type=pl.DeviceIdType.MESH
        )
    for d in (1, -1):

        @pl.when(guard(d, 0, True))
        def _(d=d):
            pl.semaphore_signal(
                barrier,
                inc=1,
                device_id={"row": r + d, "col": c},
                device_id_type=pl.DeviceIdType.MESH,
            )

    half = f_ref.shape[1] // RB_DEV
    loads[0].wait()
    loads[1].wait()
    for s in range(SUPERS):
        lower = f_ref[s, :half, :]
        mc[r, s] = jnp.where(
            pat[s, RB_DEV * r + 1] > 0,
            f_ref[s, half:, :],
            jnp.where(pat[s, RB_DEV * r] > 0, lower, jnp.zeros_like(lower)),
        )
    loads[2].wait()
    for s in range(SUPERS):
        rows = jnp.where(pat[s, RB_DEV * r + 1] > 0, a_ref[half:, :], a_ref[:half, :])
        ac[r, c, s] = jnp.where(pat[s, RB_DEV * c + 1] > 0, rows[:, half:], rows[:, :half])
    af[c] = a_ref[...]

    pl.semaphore_wait(barrier, 2 + (r > 0).astype(jnp.int32) + (r < n - 1).astype(jnp.int32))

    items = ("a", 0, 1)

    def send(item, d, t):
        (z_a(d, t) if item == "a" else z_m(d, t, item)).start()

    for item in items:
        for d in (1, -1):

            @pl.when(guard(d, 0, True))
            def _(d=d, item=item):
                send(item, d, 0)

    plane_a(1).start()
    plane_a(0).start()

    @pl.when(is_root)
    def _():
        for s in range(SUPERS):
            plane_m(r, own, s, 1).start()
            plane_m(r, own, s, 0).start()
        mr[r] = mc[r]

    def arrive(item, d, t):
        b, k = r - d * (t + 1), slot(d, t)

        @pl.when(guard(d, t, False))
        def _():
            (z_a_in(d, t) if item == "a" else z_m_in(d, t, item)).wait_recv()
            if t + 1 < n - 1:

                @pl.when(guard(d, t + 1, True))
                def _():
                    send(item, d, t + 1)

            if item == "a":
                plane_c(b, k, 1).start()
                plane_c(b, k, 0).start()
            else:

                @pl.when(is_root)
                def _():
                    plane_m(b, k, item, 1).start()
                    plane_m(b, k, item, 0).start()

    def relay(item, d, t):
        b, k = r - d * (t + 1), slot(d, t)
        if item == "a":

            @pl.when(guard(d, t, False))
            def _():
                plane_c_in(b, k, 1).wait_recv()
                plane_c(b, k, 2).start()

        else:

            @pl.when(jnp.logical_and(is_hop, guard(d, t, False)))
            def _():
                plane_m_in(b, k, item).wait_recv()
                plane_m_on(b, k, item).start()

    def relay_own():
        plane_a_in(1).wait_recv()
        plane_a(2).start()

        @pl.when(is_hop)
        def _():
            for s in range(SUPERS):
                plane_m_in(r, own, s).wait_recv()
                plane_m_on(r, own, s).start()

    events = [(item, t) for t in range(n - 1) for item in items]
    waiting = [None]
    for item, t in events:
        for d in (1, -1):
            arrive(item, d, t)
        waiting.append((item, t))
        if len(waiting) > 2:
            late = waiting.pop(0)
            if late is None:
                relay_own()
            else:
                for d in (1, -1):
                    relay(late[0], d, late[1])
    for late in waiting:
        for d in (1, -1):
            relay(late[0], d, late[1])

    plane_a_in(0).wait_recv()
    plane_a_in(2).wait_recv()
    width = mc.shape[3]
    depth = n * half
    for s in range(SUPERS):
        columns = mc[:, s].reshape(depth, width)
        left = jnp.concatenate(
            [
                jnp.where(pat[s, RB_DEV * g + 1] > 0, af[g, :, half:], af[g, :, :half])
                for g in range(n)
            ],
            axis=1,
        )
        x = jnp.dot(left, columns, preferred_element_type=jnp.float32)
        kc_ref[s] = (-x).T.astype(jnp.bfloat16)
        y[r, s] = jnp.where(pat[s, RB_DEV * r + 1] > 0, x[half:], x[:half]).astype(jnp.bfloat16)

    for d, t in steps:
        b, k = r - d * (t + 1), slot(d, t)

        @pl.when(guard(d, t, False))
        def _(b=b, k=k):
            plane_c_in(b, k, 0).wait_recv()
            plane_c_in(b, k, 2).wait_recv()

    for off in range(1, n):
        b = lax.rem(r + off, n)
        for s in range(SUPERS):
            left = jnp.concatenate([ac[b, g, s] for g in range(n)], axis=1)
            y[b, s] = jnp.dot(
                left, mc[:, s].reshape(depth, width), preferred_element_type=jnp.float32
            ).astype(jnp.bfloat16)

    @pl.when(is_root)
    def _():
        for off in range(1, n):
            b = lax.rem(r + off, n)
            mr[b] = mc[b]

    is_leaf = jnp.logical_and(jnp.logical_not(is_root), jnp.logical_not(is_hop))

    @pl.when(is_leaf)
    def _():
        for s in range(SUPERS):
            plane_m_in(r, own, s).wait_recv()

    for d, t in steps:
        b, k = r - d * (t + 1), slot(d, t)

        @pl.when(jnp.logical_and(is_leaf, guard(d, t, False)))
        def _(b=b, k=k):
            for s in range(SUPERS):
                plane_m_in(b, k, s).wait_recv()

    loads[3].wait()
    for s in range(SUPERS):
        kk_ref[s] = kk_ref[s] + lax.dot_general(
            mr[:, s].reshape(depth, width),
            y[:, s].reshape(depth, width),
            (((0,), (0,)), ((), ())),
            preferred_element_type=jnp.float32,
        )

    for d, t in steps:

        @pl.when(guard(d, t, True))
        def _(d=d, t=t):
            for s in range(SUPERS):
                z_m(d, t, s).wait_send()
            z_a(d, t).wait_send()

        @pl.when(guard(d, t, False))
        def _(d=d, t=t):
            b, k = r - d * (t + 1), slot(d, t)
            for j in range(3):
                plane_c(b, k, j).wait_send()

            @pl.when(is_root)
            def _():
                for s in range(SUPERS):
                    plane_m(b, k, s, 0).wait_send()
                    plane_m(b, k, s, 1).wait_send()

            @pl.when(is_hop)
            def _():
                for s in range(SUPERS):
                    plane_m_on(b, k, s).wait_send()

    for j in range(3):
        plane_a(j).wait_send()

    @pl.when(is_root)
    def _():
        for s in range(SUPERS):
            plane_m(r, own, s, 0).wait_send()
            plane_m(r, own, s, 1).wait_send()

    @pl.when(is_hop)
    def _():
        for s in range(SUPERS):
            plane_m_on(r, own, s).wait_send()


def write_out(cross_ref, diag_ref, cross_out, diag_out, sem):
    copies = [
        pltpu.make_async_copy(diag_ref, diag_out, sem.at[0]),
        pltpu.make_async_copy(cross_ref, cross_out, sem.at[1]),
    ]
    for copy in copies:
        copy.start()
    for copy in copies:
        copy.wait()


def body_kernel(n, ainv_cc, factor, inv_pivot, pattern):
    rows, width = factor.shape[1], factor.shape[2]
    half = rows // RB_DEV
    slots = 2 * (n - 1)
    vmem = pl.BlockSpec(memory_space=pltpu.VMEM)
    dma = pltpu.SemaphoreType.DMA
    cross, diag = pl.pallas_call(
        functools.partial(kernel, n),
        out_shape=(
            jax.ShapeDtypeStruct((SUPERS, width, rows), jnp.bfloat16),
            jax.ShapeDtypeStruct(inv_pivot.shape, jnp.float32),
        ),
        in_specs=[pl.BlockSpec(memory_space=pltpu.MemorySpace.HBM)] * 4,
        out_specs=(vmem, vmem),
        scratch_shapes=[
            pltpu.SMEM(pattern.shape, jnp.int32),
            pltpu.VMEM(factor.shape, jnp.bfloat16),
            pltpu.VMEM(ainv_cc.shape, jnp.bfloat16),
            pltpu.VMEM((n, SUPERS, half, width), jnp.bfloat16),
            pltpu.VMEM((n, SUPERS, half, width), jnp.bfloat16),
            pltpu.VMEM((n,) + ainv_cc.shape, jnp.bfloat16),
            pltpu.VMEM((n, n, SUPERS, half, half), jnp.bfloat16),
            pltpu.VMEM((n, SUPERS, half, width), jnp.bfloat16),
            dma((4,)),
            dma((slots, SUPERS)), dma((slots, SUPERS)), dma((slots,)), dma((slots,)),
            dma((3,)), dma((3,)),
            dma((slots, 3)), dma((slots, 3)),
            dma((slots + 1, SUPERS, 2)), dma((slots + 1, SUPERS)),
        ],
        compiler_params=pltpu.CompilerParams(
            collective_id=0, has_side_effects=True, vmem_limit_bytes=32 << 20
        ),
        cost_estimate=pl.CostEstimate(
            flops=2 * SUPERS * 3 * width * rows * n * half,
            bytes_accessed=8 * rows * width * SUPERS,
            transcendentals=0,
        ),
    )(
        *(
            pltpu.with_memory_space_constraint(x, pltpu.MemorySpace.HBM)
            for x in (pattern, factor, ainv_cc, inv_pivot)
        )
    )


    return pl.pallas_call(
        write_out,
        out_shape=(
            jax.ShapeDtypeStruct(cross.shape, cross.dtype),
            jax.ShapeDtypeStruct(diag.shape, diag.dtype),
        ),
        in_specs=[vmem, vmem],
        out_specs=(pl.BlockSpec(memory_space=pl.ANY), pl.BlockSpec(memory_space=pl.ANY)),
        scratch_shapes=[dma((2,))],
    )(*(pltpu.with_memory_space_constraint(x, pltpu.MemorySpace.VMEM) for x in (cross, diag)))


def solution(mesh):
    placed = (P(("pole", "row"), "col"), P("pole", "row", "col"), P("pole", "row", "col"), P())
    rows, cols = mesh.shape["row"], mesh.shape["col"]
    fits = rows == cols and cols == 4
    return jax.shard_map(
        functools.partial(body_kernel, cols) if fits else body,
        mesh=mesh,
        in_specs=placed,
        out_specs=(P("pole", "col", "row"), P("pole", "row", "col")),
        check_vma=False,
    )
```

```python
import functools

import jax
import jax.numpy as jnp
from jax import lax
from jax.experimental import pallas as pl
from jax.experimental.pallas import tpu as pltpu
from jax.sharding import PartitionSpec as P

BLK = 128
SUPERS = 2
RB_DEV = 2


def spread(x, axis, root):
    mine = lax.axis_index(axis) == root
    return lax.psum(jnp.where(mine, x, jnp.zeros_like(x)), axis)


def body(ainv_cc, factor, inv_pivot, pattern):
    rows_here = factor.shape[1]
    width_part = factor.shape[2]
    per_col = lax.axis_size("row") // lax.axis_size("col")
    row_index = lax.axis_index("row")
    col_index = lax.axis_index("col")
    full_width = lax.all_gather(factor, "col", axis=2, tiled=True)
    full_cols = full_width.shape[2]
    own_marks = lax.dynamic_slice_in_dim(pattern, row_index * RB_DEV, RB_DEV, 1)
    blocks = full_width.reshape(SUPERS, RB_DEV, BLK, full_cols)
    masked = jnp.where(own_marks[:, :, None, None] > 0, blocks, jnp.zeros_like(blocks))
    local_factor = masked.reshape(SUPERS, rows_here, full_cols)
    received = []
    for section in range(per_col):
        received.append(spread(local_factor, "row", col_index * per_col + section))
    gathered_rows = jnp.concatenate(received, axis=1)
    left_list = [ainv_cc for super_index in range(SUPERS)]
    cross_list = []
    diag_list = []
    for super_index in range(SUPERS):
        rows_matrix = gathered_rows[super_index]
        operand = left_list[super_index]
        factor_rows = local_factor[super_index]

        def column_term(first_row, row_count, rows_matrix=rows_matrix, operand=operand):
            return lax.dot_general(
                rows_matrix, operand, (((0,), (1,)), ((), ())), preferred_element_type=jnp.float32
            )

        summed = lax.psum_scatter(
            column_term(jnp.int32(0), lax.axis_size("col") * width_part).astype(jnp.bfloat16),
            "col",
            scatter_dimension=0,
            tiled=True,
        ).astype(jnp.float32)
        cross_block = (-summed).astype(jnp.bfloat16)

        def diagonal_term(first_row, row_count, factor_rows=factor_rows, cross_block=cross_block):
            return lax.dot_general(
                factor_rows,
                cross_block,
                (((0,), (1,)), ((), ())),
                preferred_element_type=jnp.float32,
            )

        update = lax.psum_scatter(
            diagonal_term(
                jnp.int32(0), lax.axis_size("row") * (full_cols // lax.axis_size("row"))
            ).astype(jnp.bfloat16),
            "row",
            scatter_dimension=0,
            tiled=True,
        ).astype(jnp.float32)
        cross_list.append(cross_block)
        diag_list.append(inv_pivot[super_index] - update)
    return (jnp.stack(cross_list), jnp.stack(diag_list))


def remote(src, dst, send_sem, recv_sem, row, col):
    return pltpu.make_async_remote_copy(
        src_ref=src,
        dst_ref=dst,
        send_sem=send_sem,
        recv_sem=recv_sem,
        device_id={"row": row, "col": col},
        device_id_type=pl.DeviceIdType.MESH,
    )


def kernel(
    n, pat_hbm, f_hbm, a_hbm, p_hbm, kc_ref, kk_ref,
    pat, f_ref, a_ref, mc, mr, af, ac, y, load_sem,
    zm_send, zm_recv, za_send, za_recv, pa_send, pa_recv, pc_send, pc_recv, pm_send, pm_recv,
):
    r = lax.axis_index("row")
    c = lax.axis_index("col")
    sib = c + 1 - 2 * lax.rem(c, 2)
    far = lax.rem(c + 2, n)
    far_sib = lax.rem(sib + 2, n)
    steps = [(d, t) for t in range(n - 1) for d in (1, -1)]

    def slot(d, t):
        return t * 2 + (0 if d == 1 else 1)

    def guard(d, t, sending):
        if sending:
            if d == 1:
                return jnp.logical_and(r >= t, r < n - 1)
            return jnp.logical_and(r <= n - 1 - t, r > 0)
        if d == 1:
            return r >= t + 1
        return r <= n - 2 - t

    def z_m(d, t, s):
        b, k = r - d * t, slot(d, t)
        return remote(mc.at[b, s], mc.at[b, s], zm_send.at[k, s], zm_recv.at[k, s], r + d, c)

    def z_a(d, t):
        b, k = r - d * t, slot(d, t)
        return remote(ac.at[b, c], ac.at[b, c], za_send.at[k], za_recv.at[k], r + d, c)

    def z_m_in(d, t, s):
        b, k = r - d * (t + 1), slot(d, t)
        return remote(mc.at[b, s], mc.at[b, s], zm_send.at[k, s], zm_recv.at[k, s], r - d, c)

    def z_a_in(d, t):
        b, k = r - d * (t + 1), slot(d, t)
        return remote(ac.at[b, c], ac.at[b, c], za_send.at[k], za_recv.at[k], r - d, c)

    def plane_a(j):
        col, block = ((sib, c), (far, c), (sib, far))[j]
        return remote(af.at[block], af.at[block], pa_send.at[j], pa_recv.at[j], r, col)

    def plane_a_in(j):
        block = (sib, far, far_sib)[j]
        return remote(af.at[block], af.at[block], pa_send.at[j], pa_recv.at[j], r, sib)

    def plane_c(b, k, j):
        col, block = ((sib, c), (far, c), (sib, far))[j]
        return remote(
            ac.at[b, block], ac.at[b, block], pc_send.at[k, j], pc_recv.at[k, j], r, col
        )

    def plane_c_in(b, k, j):
        block = (sib, far, far_sib)[j]
        return remote(
            ac.at[b, block], ac.at[b, block], pc_send.at[k, j], pc_recv.at[k, j], r, sib
        )

    def plane_m(b, k, s, j):
        return remote(
            mc.at[b, s], mr.at[b, s], pm_send.at[k, s, j], pm_recv.at[k, s], r, (sib, far)[j]
        )

    def plane_m_on(b, k, s):
        return remote(mr.at[b, s], mr.at[b, s], pm_send.at[k, s, 0], pm_recv.at[k, s], r, sib)

    plane_m_in = plane_m_on

    is_root = c == r
    is_hop = far == r
    own = slot(-1, n - 2) + 1

    loads = [
        pltpu.make_async_copy(src, dst, load_sem.at[i])
        for i, (src, dst) in enumerate(
            ((pat_hbm, pat), (f_hbm, f_ref), (a_hbm, a_ref), (p_hbm, kk_ref))
        )
    ]
    for load in loads:
        load.start()

    barrier = pltpu.get_barrier_semaphore()
    for col in (sib, far):
        pl.semaphore_signal(
            barrier, inc=1, device_id={"row": r, "col": col}, device_id_type=pl.DeviceIdType.MESH
        )
    for d in (1, -1):

        @pl.when(guard(d, 0, True))
        def _(d=d):
            pl.semaphore_signal(
                barrier,
                inc=1,
                device_id={"row": r + d, "col": c},
                device_id_type=pl.DeviceIdType.MESH,
            )

    half = f_ref.shape[1] // RB_DEV
    loads[0].wait()
    loads[1].wait()
    for s in range(SUPERS):
        lower = f_ref[s, :half, :]
        mc[r, s] = jnp.where(
            pat[s, RB_DEV * r + 1] > 0,
            f_ref[s, half:, :],
            jnp.where(pat[s, RB_DEV * r] > 0, lower, jnp.zeros_like(lower)),
        )
    loads[2].wait()
    for s in range(SUPERS):
        rows = jnp.where(pat[s, RB_DEV * r + 1] > 0, a_ref[half:, :], a_ref[:half, :])
        ac[r, c, s] = jnp.where(pat[s, RB_DEV * c + 1] > 0, rows[:, half:], rows[:, :half])
    af[c] = a_ref[...]

    pl.semaphore_wait(barrier, 2 + (r > 0).astype(jnp.int32) + (r < n - 1).astype(jnp.int32))

    items = ("a", 0, 1)

    def send(item, d, t):
        (z_a(d, t) if item == "a" else z_m(d, t, item)).start()

    for item in items:
        for d in (1, -1):

            @pl.when(guard(d, 0, True))
            def _(d=d, item=item):
                send(item, d, 0)

    plane_a(1).start()
    plane_a(0).start()

    @pl.when(is_root)
    def _():
        for s in range(SUPERS):
            plane_m(r, own, s, 1).start()
            plane_m(r, own, s, 0).start()
        mr[r] = mc[r]

    def arrive(item, d, t):
        b, k = r - d * (t + 1), slot(d, t)

        @pl.when(guard(d, t, False))
        def _():
            (z_a_in(d, t) if item == "a" else z_m_in(d, t, item)).wait_recv()
            if t + 1 < n - 1:

                @pl.when(guard(d, t + 1, True))
                def _():
                    send(item, d, t + 1)

            if item == "a":
                plane_c(b, k, 1).start()
                plane_c(b, k, 0).start()
            else:

                @pl.when(is_root)
                def _():
                    plane_m(b, k, item, 1).start()
                    plane_m(b, k, item, 0).start()

    def relay(item, d, t):
        b, k = r - d * (t + 1), slot(d, t)
        if item == "a":

            @pl.when(guard(d, t, False))
            def _():
                plane_c_in(b, k, 1).wait_recv()
                plane_c(b, k, 2).start()

        else:

            @pl.when(jnp.logical_and(is_hop, guard(d, t, False)))
            def _():
                plane_m_in(b, k, item).wait_recv()
                plane_m_on(b, k, item).start()

    def relay_own():
        plane_a_in(1).wait_recv()
        plane_a(2).start()

        @pl.when(is_hop)
        def _():
            for s in range(SUPERS):
                plane_m_in(r, own, s).wait_recv()
                plane_m_on(r, own, s).start()

    events = [(item, t) for t in range(n - 1) for item in items]
    waiting = [None]
    for item, t in events:
        for d in (1, -1):
            arrive(item, d, t)
        waiting.append((item, t))
        if len(waiting) > 2:
            late = waiting.pop(0)
            if late is None:
                relay_own()
            else:
                for d in (1, -1):
                    relay(late[0], d, late[1])
    for late in waiting[:-1]:
        for d in (1, -1):
            relay(late[0], d, late[1])

    plane_a_in(0).wait_recv()
    plane_a_in(2).wait_recv()
    width = mc.shape[3]
    depth = n * half
    for s in range(SUPERS):
        columns = mc[:, s].reshape(depth, width)
        left = jnp.concatenate(
            [
                jnp.where(pat[s, RB_DEV * g + 1] > 0, af[g, :, half:], af[g, :, :half])
                for g in range(n)
            ],
            axis=1,
        )
        x = jnp.dot(left, columns, preferred_element_type=jnp.float32)
        kc_ref[s] = (-x).T.astype(jnp.bfloat16)
        y[r, s] = jnp.where(pat[s, RB_DEV * r + 1] > 0, x[half:], x[:half]).astype(jnp.bfloat16)

    for d in (1, -1):
        relay(waiting[-1][0], d, waiting[-1][1])

    @pl.when(is_root)
    def _():
        for off in range(1, n):
            b = lax.rem(r + off, n)
            mr[b] = mc[b]

    for d, t in steps:
        b, k = r - d * (t + 1), slot(d, t)

        @pl.when(guard(d, t, False))
        def _(b=b, k=k):
            plane_c_in(b, k, 0).wait_recv()
            plane_c_in(b, k, 2).wait_recv()

    for off in range(1, n):
        b = lax.rem(r + off, n)
        for s in range(SUPERS):
            left = jnp.concatenate([ac[b, g, s] for g in range(n)], axis=1)
            y[b, s] = jnp.dot(
                left, mc[:, s].reshape(depth, width), preferred_element_type=jnp.float32
            ).astype(jnp.bfloat16)

    is_leaf = jnp.logical_and(jnp.logical_not(is_root), jnp.logical_not(is_hop))

    @pl.when(is_leaf)
    def _():
        for s in range(SUPERS):
            plane_m_in(r, own, s).wait_recv()

    for d, t in steps:
        b, k = r - d * (t + 1), slot(d, t)

        @pl.when(jnp.logical_and(is_leaf, guard(d, t, False)))
        def _(b=b, k=k):
            for s in range(SUPERS):
                plane_m_in(b, k, s).wait_recv()

    loads[3].wait()
    for s in range(SUPERS):
        kk_ref[s] = kk_ref[s] + lax.dot_general(
            mr[:, s].reshape(depth, width),
            y[:, s].reshape(depth, width),
            (((0,), (0,)), ((), ())),
            preferred_element_type=jnp.float32,
        )

    for d, t in steps:

        @pl.when(guard(d, t, True))
        def _(d=d, t=t):
            for s in range(SUPERS):
                z_m(d, t, s).wait_send()
            z_a(d, t).wait_send()

        @pl.when(guard(d, t, False))
        def _(d=d, t=t):
            b, k = r - d * (t + 1), slot(d, t)
            for j in range(3):
                plane_c(b, k, j).wait_send()

            @pl.when(is_root)
            def _():
                for s in range(SUPERS):
                    plane_m(b, k, s, 0).wait_send()
                    plane_m(b, k, s, 1).wait_send()

            @pl.when(is_hop)
            def _():
                for s in range(SUPERS):
                    plane_m_on(b, k, s).wait_send()

    for j in range(3):
        plane_a(j).wait_send()

    @pl.when(is_root)
    def _():
        for s in range(SUPERS):
            plane_m(r, own, s, 0).wait_send()
            plane_m(r, own, s, 1).wait_send()

    @pl.when(is_hop)
    def _():
        for s in range(SUPERS):
            plane_m_on(r, own, s).wait_send()


def write_out(cross_ref, diag_ref, cross_out, diag_out, sem):
    copies = [
        pltpu.make_async_copy(diag_ref, diag_out, sem.at[0]),
        pltpu.make_async_copy(cross_ref, cross_out, sem.at[1]),
    ]
    for copy in copies:
        copy.start()
    for copy in copies:
        copy.wait()


def body_kernel(n, ainv_cc, factor, inv_pivot, pattern):
    rows, width = factor.shape[1], factor.shape[2]
    half = rows // RB_DEV
    slots = 2 * (n - 1)
    vmem = pl.BlockSpec(memory_space=pltpu.VMEM)
    dma = pltpu.SemaphoreType.DMA
    cross, diag = pl.pallas_call(
        functools.partial(kernel, n),
        out_shape=(
            jax.ShapeDtypeStruct((SUPERS, width, rows), jnp.bfloat16),
            jax.ShapeDtypeStruct(inv_pivot.shape, jnp.float32),
        ),
        in_specs=[pl.BlockSpec(memory_space=pltpu.MemorySpace.HBM)] * 4,
        out_specs=(vmem, vmem),
        scratch_shapes=[
            pltpu.SMEM(pattern.shape, jnp.int32),
            pltpu.VMEM(factor.shape, jnp.bfloat16),
            pltpu.VMEM(ainv_cc.shape, jnp.bfloat16),
            pltpu.VMEM((n, SUPERS, half, width), jnp.bfloat16),
            pltpu.VMEM((n, SUPERS, half, width), jnp.bfloat16),
            pltpu.VMEM((n,) + ainv_cc.shape, jnp.bfloat16),
            pltpu.VMEM((n, n, SUPERS, half, half), jnp.bfloat16),
            pltpu.VMEM((n, SUPERS, half, width), jnp.bfloat16),
            dma((4,)),
            dma((slots, SUPERS)), dma((slots, SUPERS)), dma((slots,)), dma((slots,)),
            dma((3,)), dma((3,)),
            dma((slots, 3)), dma((slots, 3)),
            dma((slots + 1, SUPERS, 2)), dma((slots + 1, SUPERS)),
        ],
        compiler_params=pltpu.CompilerParams(
            collective_id=0, has_side_effects=True, vmem_limit_bytes=32 << 20
        ),
        cost_estimate=pl.CostEstimate(
            flops=2 * SUPERS * 3 * width * rows * n * half,
            bytes_accessed=8 * rows * width * SUPERS,
            transcendentals=0,
        ),
    )(
        *(
            pltpu.with_memory_space_constraint(x, pltpu.MemorySpace.HBM)
            for x in (pattern, factor, ainv_cc, inv_pivot)
        )
    )


    return pl.pallas_call(
        write_out,
        out_shape=(
            jax.ShapeDtypeStruct(cross.shape, cross.dtype),
            jax.ShapeDtypeStruct(diag.shape, diag.dtype),
        ),
        in_specs=[vmem, vmem],
        out_specs=(pl.BlockSpec(memory_space=pl.ANY), pl.BlockSpec(memory_space=pl.ANY)),
        scratch_shapes=[dma((2,))],
    )(*(pltpu.with_memory_space_constraint(x, pltpu.MemorySpace.VMEM) for x in (cross, diag)))


def solution(mesh):
    placed = (P(("pole", "row"), "col"), P("pole", "row", "col"), P("pole", "row", "col"), P())
    rows, cols = mesh.shape["row"], mesh.shape["col"]
    fits = rows == cols and cols == 4
    return jax.shard_map(
        functools.partial(body_kernel, cols) if fits else body,
        mesh=mesh,
        in_specs=placed,
        out_specs=(P("pole", "col", "row"), P("pole", "row", "col")),
        check_vma=False,
    )
```
